32 devices in a mesh: dp: 8 (over z, y), tensor: 4 (over x, core).
Axes of the slice: x: 2, y: 2, z: 4, core: 2. Of those that a mesh axis runs over, the one named last changes fastest.
Arguments:
- layer_input: bfloat16 [4096, 16384], P('dp', 'tensor'), may hold values from -6 to 6
- queries: bfloat16 [4096, 4096], P('dp', 'tensor'), may hold values from -128 to 128
- key_value: bfloat16 [4096, 512], P('dp', 'tensor'), may hold values from -16 to 16
- out_grad: bfloat16 [4096, 4096], P('dp', 'tensor'), may hold values from -6 to 6
- segment_ids: int32 [8, 512], P('dp'), may hold values from 0 to 63, as said below
Outputs:
- grad_query: bfloat16 [4096, 4096], P('dp', 'tensor')
- grad_key_value: bfloat16 [4096, 512], P('dp', 'tensor')
- grad_weights: bfloat16 [16384, 512], P(('tensor', 'dp'))
The draws below stay inside these ranges and needn't reach their ends.
Inputs may be any that keep to these rules, and one draw needn't show every extreme that they name: `segment_ids`: along each sequence the ids start at 0, never fall, and rise by one at most, only at positions that are multiples of 8.
All inputs are finite; a program needn't handle non-finite values.
Results may differ from the reference program's by a relative error of at most 0.017.
Values may be sent and summed in bfloat16 or wider, within the bound.
A program may use at most 128 MiB of HBM per device.

```python
import math
import jax
import jax.numpy as jnp
from jax import lax

D = 16384
HD = 128
TOK_DEV = 512
GROUP = 16
HEADS = 32
KV_HEADS = 2
SEQS = 8
TOKENS = 4096


def segment_starts(key):
    start_draw = jax.random.randint(jax.random.fold_in(key, 31), (SEQS, TOK_DEV), 0, 6)
    forced_row = jax.random.randint(jax.random.fold_in(key, 32), (), 0, SEQS)
    position = jnp.arange(TOK_DEV)[None, :]
    row_index = jnp.arange(SEQS)[:, None]
    on_grid = position % 8 == 0
    return on_grid & ((start_draw == 0) | (row_index == forced_row)) | (position == 0)


def draw_segment_ids(key, part):
    starts = segment_starts(key).astype(jnp.int32)
    return (jnp.cumsum(starts, axis=1) - 1).astype(jnp.int32)


def drawn_parts(key):
    full_shape = (TOKENS, KV_HEADS, 2, HD)
    base_key = jax.random.fold_in(key, 41)
    base_draw = jax.random.truncated_normal(base_key, -4.5, 4.5, full_shape, jnp.float32)
    row_scale = jnp.exp(jax.random.uniform(jax.random.fold_in(key, 42), (TOKENS, 1, 1, 1), jnp.float32, math.log(0.4), math.log(4.0)))
    pair_rows = base_draw * row_scale
    return pair_rows


def draw_key_value(key, part):
    pair_rows = drawn_parts(key)
    return jnp.clip(pair_rows, -16.0, 16.0).reshape(TOKENS, KV_HEADS * 2 * HD).astype(jnp.bfloat16)


def draw_queries(key, part):
    full_shape = (TOKENS, KV_HEADS, GROUP, HD)
    base_key = jax.random.fold_in(key, 51)
    row_scale = jnp.exp(jax.random.uniform(jax.random.fold_in(key, 52), (TOKENS, 1, 1, 1), jnp.float32, math.log(0.5), math.log(2.0)))
    base_draw = jax.random.truncated_normal(base_key, -4.5, 4.5, full_shape, jnp.float32) * row_scale
    return jnp.clip(base_draw, -128.0, 128.0).reshape(TOKENS, KV_HEADS * GROUP * HD).astype(jnp.bfloat16)


def with_spikes(values, rng, source, target, parts, factor):
    def block_of(axis_at):
        return (jnp.arange(values.shape[axis_at]) // (values.shape[axis_at] // parts)).reshape((-1,) + (1,) * (values.ndim - 1 - axis_at))

    near = jax.random.permutation(rng, parts)[block_of(target)]
    second = (block_of(target) + parts // 2) % parts
    return jnp.where((block_of(source) == near) | (block_of(source) == second), factor * values, values)


def block_levels(own_key, extent, split, least, top_value):
    gain = 1.0
    for dim, parts in split:
        draws = jax.random.uniform(jax.random.fold_in(jax.random.fold_in(own_key, 6), dim), (parts,), jnp.float32, least / len(split), top_value / len(split))
        gain = gain * jnp.repeat(jnp.exp(draws), extent[dim] // parts).reshape((-1,) + (1,) * (len(extent) - 1 - dim))
    return gain


def centred(own_key, dims, spread, limit, shards=(), dtype=jnp.bfloat16):
    drawn = spread * jax.random.normal(own_key, dims, jnp.float32)
    if shards:
        drawn = drawn * block_levels(own_key, dims, shards, -0.22, 0.18)
    return jnp.clip(drawn, -limit, limit).astype(dtype)


def heavy_noise(rng, shape, scale, bound, cuts, heavy, held_as=jnp.bfloat16):
    result = scale * jax.random.normal(rng, shape, jnp.float32)
    if cuts:
        result = result * block_levels(rng, shape, cuts, -0.22, 0.18)
    return jnp.clip(with_spikes(result, jax.random.fold_in(rng, 3), *heavy), -bound, bound).astype(held_as)


def setup_inputs(seed: int = 0) -> dict:
    key_of = jax.random.split(jax.random.key(seed), 6)
    return {
        "layer_input": heavy_noise(key_of[0], (TOKENS, D), 1.0, 6.0, ((0, 8), (1, 4)), (0, 1, 8, 2.0)),
        "queries": draw_queries(jax.random.fold_in(key_of[5], 71), 0),
        "key_value": draw_key_value(jax.random.fold_in(key_of[5], 71), 0),
        "out_grad": centred(key_of[3], (TOKENS, HEADS * HD), 1.0, 6.0, ((0, 8), (1, 4))),
        "segment_ids": draw_segment_ids(jax.random.fold_in(key_of[5], 71), 0),
    }


def backward_one(seq_items):
    query_seq, pair_seq, grad_seq, segment_row = seq_items
    score_scale = HD ** -0.5
    key_rows = pair_seq[:, :, 0, :].astype(jnp.float32)
    value_rows = pair_seq[:, :, 1, :].astype(jnp.float32)
    query_float = query_seq.astype(jnp.float32)
    grad_float = grad_seq.astype(jnp.float32)
    position = jnp.arange(TOK_DEV)
    allowed = (position[None, :] <= position[:, None]) & (segment_row[:, None] == segment_row[None, :])
    scores = jnp.einsum("tgnd,sgd->gnts", query_float, key_rows) * score_scale
    scores = jnp.where(allowed, scores, -1e30)
    row_max = jnp.max(scores, axis=-1, keepdims=True)
    weights = jnp.exp(scores - row_max)
    probability = weights / jnp.sum(weights, axis=-1, keepdims=True)
    prob_rounded = lax.optimization_barrier(probability.astype(jnp.bfloat16)).astype(jnp.float32)
    attended = jnp.einsum("gnts,sgd->gntd", prob_rounded, value_rows)
    row_delta = jnp.einsum("tgnd,gntd->gnt", grad_float, attended)
    prob_grad = jnp.einsum("tgnd,sgd->gnts", grad_float, value_rows)
    score_grad = probability * (prob_grad - row_delta[..., None])
    score_rounded = lax.optimization_barrier(score_grad.astype(jnp.bfloat16)).astype(jnp.float32)
    query_part = (jnp.einsum("gnts,sgd->tgnd", score_rounded, key_rows) * score_scale).astype(jnp.bfloat16)
    key_part = jnp.einsum("gnts,tgnd->sgd", score_rounded, query_float) * score_scale
    value_part = jnp.einsum("gnts,tgnd->sgd", prob_rounded, grad_float)
    pair_grad = jnp.stack([key_part, value_part], axis=2).astype(jnp.bfloat16)
    return query_part.reshape(TOK_DEV, KV_HEADS * GROUP * HD), pair_grad.reshape(TOK_DEV, KV_HEADS * 2 * HD)


def reference(layer_input, queries, key_value, out_grad, segment_ids):
    query_all = queries.reshape(SEQS, TOK_DEV, KV_HEADS, GROUP, HD)
    pair_all = key_value.reshape(SEQS, TOK_DEV, KV_HEADS, 2, HD)
    grad_all = out_grad.reshape(SEQS, TOK_DEV, KV_HEADS, GROUP, HD)
    grad_query, grad_pairs = lax.map(backward_one, (query_all, pair_all, grad_all, segment_ids))
    input_seqs = layer_input.reshape(SEQS, TOK_DEV, D)

    def add_term(running_sum, term_items):
        input_seq, pair_seq = term_items
        term = jnp.dot(input_seq.T, pair_seq, preferred_element_type=jnp.float32) / SEQS
        term = lax.optimization_barrier(term.astype(jnp.bfloat16)).astype(jnp.float32)
        return running_sum + term, None

    summed, unused = lax.scan(add_term, jnp.zeros((D, KV_HEADS * 2 * HD), jnp.float32), (input_seqs, grad_pairs))
    return (grad_query.reshape(TOKENS, KV_HEADS * GROUP * HD),
            grad_pairs.reshape(TOKENS, KV_HEADS * 2 * HD),
            summed.astype(jnp.bfloat16))
```

```python
import functools
import math
import jax
import jax.numpy as jnp
from jax import lax
from jax.experimental import pallas as pl
from jax.experimental.pallas import tpu as pltpu
from jax.sharding import PartitionSpec as P

F32 = jnp.float32
BF16 = jnp.bfloat16


def nt(a, b):
    return lax.dot_general(a, b, (((1,), (1,)), ((), ())), preferred_element_type=F32)


def nn(a, b):
    return lax.dot_general(a, b, (((1,), (0,)), ((), ())), preferred_element_type=F32)


def tn(a, b):
    return lax.dot_general(a, b, (((0,), (0,)), ((), ())), preferred_element_type=F32)


def kernel(
    nd,
    nt_dev,
    feat,
    li_hbm,
    q_ref,
    kv_ref,
    og_ref,
    seg_ref,
    dq_ref,
    gkv_ref,
    gw_ref,
    kv_in,
    bias,
    kt,
    acc_k,
    acc_v,
    part_out,
    part_in,
    gbuf,
    li,
    pacc,
    sbuf,
    rbuf,
    kv_sem,
    lo_sem,
    ls_sem,
    lr_sem,
    px_sem,
    y_sem,
    fwd_sem,
    loc_sem,
    xs_sem,
    xr_sem,
    cs_sem,
    cr_sem,
):
    tok, hd = kv_ref.shape
    heads = q_ref.shape[1] // hd
    n = nd // 2
    groups = nt_dev // 2
    dp = lax.axis_index("dp")
    te = lax.axis_index("tensor")
    z = dp // 2
    y = dp % 2
    c = te % 2
    grp = te // 2
    other_y = z * 2 + 1 - y
    mate = grp * 2 + 1 - c

    def remote(src, dst, ssem, rsem, d, t):
        return pltpu.make_async_remote_copy(
            src_ref=src,
            dst_ref=dst,
            send_sem=ssem,
            recv_sem=rsem,
            device_id={"dp": d, "tensor": t},
            device_id_type=pl.DeviceIdType.MESH,
        )

    barrier = pltpu.get_barrier_semaphore()
    pl.semaphore_signal(
        barrier, inc=1, device_id={"dp": other_y, "tensor": te}, device_id_type=pl.DeviceIdType.MESH
    )
    for step in (1, n - 1):
        pl.semaphore_signal(
            barrier,
            inc=1,
            device_id={"dp": ((z + step) % n) * 2 + y, "tensor": te},
            device_id_type=pl.DeviceIdType.MESH,
        )
    for step in range(1, nt_dev):
        pl.semaphore_signal(
            barrier,
            inc=1,
            device_id={"dp": dp, "tensor": (te + step) % nt_dev},
            device_id_type=pl.DeviceIdType.MESH,
        )
    pl.semaphore_wait(barrier, 3 + nt_dev - 1)

    kv_copy = remote(kv_ref, kv_in, kv_sem.at[0], kv_sem.at[1], dp, mate)
    kv_copy.start()

    def feat_at(zz, yy):
        return li_hbm.at[:, pl.ds(pl.multiple_of((zz * 2 + yy) * feat, feat), feat)]

    def li_remote(zz):
        return remote(
            feat_at(zz, 1 - y),
            li.at[zz, pl.ds(tok, tok), :],
            ls_sem.at[zz],
            lr_sem.at[zz],
            other_y,
            te,
        )

    def li_local(zz):
        return pltpu.make_async_copy(feat_at(zz, y), li.at[zz, pl.ds(0, tok), :], lo_sem.at[zz])

    def li_order(k):
        low = n - 1 - k
        low = jnp.where(low <= z, low - 1, low)
        high = jnp.where(k >= z, k + 1, k)
        v = jnp.where(z < n // 2, low, high)
        return jnp.where(k == n - 1, z, v)

    for k in range(n):
        li_remote(li_order(k)).start()
    for k in range(n):
        li_local(k).start()

    seg_b = jnp.broadcast_to(seg_ref[...].astype(F32), (tok, tok))
    key_pos = lax.broadcasted_iota(jnp.int32, (tok, tok), 0)
    qry_pos = lax.broadcasted_iota(jnp.int32, (tok, tok), 1)
    allowed = (key_pos <= qry_pos) & (seg_b.T == seg_b)
    bias[...] = jnp.where(allowed, 0.0, -1e30).astype(F32)
    acc_k[...] = jnp.zeros_like(acc_k)
    acc_v[...] = jnp.zeros_like(acc_v)
    kv_copy.wait()
    even = c == 0
    keys = jnp.where(even, kv_ref[...], kv_in[...])
    values = jnp.where(even, kv_in[...], kv_ref[...])
    scale = hd**-0.5
    coef = scale * math.log2(math.e)
    kt[0] = keys
    kt[1] = values
    keys_t = keys.astype(F32).T.astype(BF16)
    blk = tok // 2

    def head(h, carry):
        cols = pl.ds(pl.multiple_of(h * hd, hd), hd)
        for b in range(2):
            rows = pl.ds(b * blk, blk)
            kc = (b + 1) * blk
            q = q_ref[rows, cols]
            o = og_ref[rows, cols]
            s = nt(kt[0, 0:kc, :], q) * coef + bias[0:kc, rows]
            m = jnp.max(s, axis=0, keepdims=True)
            w = jnp.exp2(s - m)
            inv = 1.0 / jnp.sum(w, axis=0, keepdims=True)
            prob = w * inv
            pb = prob.astype(BF16)
            dpr = nt(kt[1, 0:kc, :], o)
            delta = jnp.sum(pb.astype(F32) * dpr, axis=0, keepdims=True)
            ds = (prob * (dpr - delta)).astype(BF16)
            acc_v[0:kc, :] += nn(pb, o)
            acc_k[0:kc, :] += nn(ds, q)
            dqt = nn(keys_t[:, 0:kc], ds) * scale
            dq_ref[rows, cols] = dqt.T.astype(BF16)
        return carry

    lax.fori_loop(0, heads, head, 0)

    dk = acc_k[...] * scale
    dv = acc_v[...]
    part_out[...] = jnp.where(even, dv, dk).astype(BF16)
    px = remote(part_out, part_in, px_sem.at[0], px_sem.at[1], dp, mate)
    px.start()
    mine = jnp.where(even, dk, dv)
    px.wait()
    gkv_ref[...] = (mine + part_in[...].astype(F32)).astype(BF16)

    def cell(r, half, core):
        lanes = pl.ds(pl.multiple_of(core * hd, hd), hd)
        return gbuf.at[r, pl.ds(half * tok, tok), lanes]

    own = pltpu.make_async_copy(gkv_ref, cell(0, 0, c), loc_sem)
    own.start()
    y_copy = remote(gkv_ref, cell(0, 1, c), y_sem.at[0], y_sem.at[1], other_y, te)
    y_copy.start()
    fwd0 = remote(gkv_ref, cell(0, 0, c), fwd_sem.at[0, 0], fwd_sem.at[1, 0], dp, mate)
    fwd0.start()

    def x_copy(r, core, half, src):
        back = groups - r
        return remote(
            src,
            cell(back, half, c),
            xs_sem.at[r, core, half],
            xr_sem.at[back, c, half],
            dp,
            ((grp + r) % groups) * 2 + core,
        )

    for r in range(1, groups):
        for core in range(2):
            x_copy(r, core, 0, gkv_ref).start()
    y_copy.wait_recv()
    fwd1 = remote(cell(0, 1, c), cell(0, 1, c), fwd_sem.at[0, 1], fwd_sem.at[1, 1], dp, mate)
    fwd1.start()
    for r in range(1, groups):
        for core in range(2):
            x_copy(r, core, 1, cell(0, 1, c)).start()
    own.wait()
    y_copy.wait_send()
    for half, copy in ((0, fwd0), (1, fwd1)):
        copy.wait_send()
        land = cell(0, half, 1 - c)
        remote(land, land, fwd_sem.at[0, half], fwd_sem.at[1, half], dp, mate).wait_recv()

    inv_seq = 1.0 / nd

    def product(r, zz):
        pacc[...] = tn(li[zz], gbuf[r]) * inv_seq

    def chain(side, r, zz):
        step = 1 if side == 0 else -1
        return remote(
            sbuf.at[side, r, zz],
            rbuf.at[side, r, zz],
            cs_sem.at[side, r, zz],
            cr_sem.at[side, r, zz],
            (z + step) * 2 + y,
            te,
        )

    def li_wait(zz):
        li_local(zz).wait()
        li_remote(zz).wait_recv()

    def arrived(side, r, zz):
        return remote(
            sbuf.at[side, r, zz],
            rbuf.at[side, r, zz],
            cs_sem.at[side, r, zz],
            cr_sem.at[side, r, zz],
            ((z + 1) % n) * 2 + y,
            te,
        )

    def hop(side, r, zz):
        @pl.when(r == 0)
        def _():
            li_wait(zz)

        product(r, zz)
        inner = (z > 0) if side == 0 else (z < n - 1)

        @pl.when(inner)
        def _():
            arrived(side, r, zz).wait_recv()
            pacc[...] += rbuf[side, r, zz].astype(F32)

        sbuf[side, r, zz] = pacc[...].astype(BF16)
        chain(side, r, zz).start()

    def group_step(r, carry):
        @pl.when(r > 0)
        def _():
            for core in range(2):
                for half in range(2):
                    land = cell(r, half, core)
                    remote(
                        land, land, xs_sem.at[r, core, half], xr_sem.at[r, core, half], dp, mate
                    ).wait_recv()

        def dist_step(k, carry):
            right = n - 1 - k

            @pl.when(right > z)
            def _():
                hop(0, r, right)

            @pl.when(k < z)
            def _():
                hop(1, r, k)

            return carry

        return lax.fori_loop(0, n - 1, dist_step, carry)

    lax.fori_loop(0, groups, group_step, 0)
    li_wait(z)

    def finish(r, carry):
        product(r, z)

        @pl.when(z > 0)
        def _():
            arrived(0, r, z).wait_recv()
            pacc[...] += rbuf[0, r, z].astype(F32)

        @pl.when(z < n - 1)
        def _():
            arrived(1, r, z).wait_recv()
            pacc[...] += rbuf[1, r, z].astype(F32)

        width = 2 * hd
        at = pl.multiple_of(((grp + r) % groups) * width, width)
        gw_ref[:, pl.ds(at, width)] = pacc[...].astype(BF16)
        return carry

    lax.fori_loop(0, groups, finish, 0)

    for k in range(n):
        li_remote(k).wait_send()
    for r in range(1, groups):
        for core in range(2):
            for half in range(2):
                x_copy(r, core, half, cell(0, half, c)).wait_send()

    def drain(r, carry):
        def drain_step(k, carry):
            right = n - 1 - k

            @pl.when(right > z)
            def _():
                arrived(0, r, right).wait_send()

            @pl.when(k < z)
            def _():
                arrived(1, r, k).wait_send()

            return carry

        return lax.fori_loop(0, n - 1, drain_step, carry)

    lax.fori_loop(0, groups, drain, 0)


def fused(nd, nt_dev, layer_input, queries, key_value, out_grad, segment_ids):
    tok, hd = key_value.shape
    feat = layer_input.shape[1] // nd
    n, groups = nd // 2, nt_dev // 2
    width = 2 * hd
    vmem = pl.BlockSpec(memory_space=pltpu.VMEM)
    dma = pltpu.SemaphoreType.DMA
    return pl.pallas_call(
        functools.partial(kernel, nd, nt_dev, feat),
        out_shape=(
            jax.ShapeDtypeStruct(queries.shape, BF16),
            jax.ShapeDtypeStruct(key_value.shape, BF16),
            jax.ShapeDtypeStruct((feat, width * groups), BF16),
        ),
        in_specs=[pl.BlockSpec(memory_space=pl.ANY), vmem, vmem, vmem, vmem],
        out_specs=(vmem, vmem, vmem),
        scratch_shapes=[
            pltpu.VMEM((tok, hd), BF16),
            pltpu.VMEM((tok, tok), F32),
            pltpu.VMEM((2, tok, hd), BF16),
            pltpu.VMEM((tok, hd), F32),
            pltpu.VMEM((tok, hd), F32),
            pltpu.VMEM((tok, hd), BF16),
            pltpu.VMEM((tok, hd), BF16),
            pltpu.VMEM((groups, 2 * tok, width), BF16),
            pltpu.VMEM((n, 2 * tok, feat), BF16),
            pltpu.VMEM((feat, width), F32),
            pltpu.VMEM((2, groups, n, feat, width), BF16),
            pltpu.VMEM((2, groups, n, feat, width), BF16),
            dma((2,)),
            dma((n,)),
            dma((n,)),
            dma((n,)),
            dma((2,)),
            dma((2,)),
            dma((2, 2)),
            dma,
            dma((groups, 2, 2)),
            dma((groups, 2, 2)),
            dma((2, groups, n)),
            dma((2, groups, n)),
        ],
        compiler_params=pltpu.CompilerParams(
            collective_id=0, has_side_effects=True, vmem_limit_bytes=56 * 2**20
        ),
    )(layer_input, queries, key_value, out_grad, segment_ids)


def partner_2(value, axis, stride):
    mask = 2**stride
    pairs = [(source, source ^ mask) for source in range(lax.axis_size(axis))]
    return lax.ppermute(value, axis, pairs)


def score_block(query_block, grad_block, key_rows, value_rows, allowed, score_scale):
    scores = (
        jnp.einsum("thd,sd->hts", query_block, key_rows, preferred_element_type=jnp.float32)
        * score_scale
    )
    scores = jnp.where(allowed[None], scores, -1e30)
    row_max = jnp.max(scores, axis=-1, keepdims=True)
    weights = jnp.exp(scores - row_max)
    probability = weights / jnp.sum(weights, axis=-1, keepdims=True)
    prob_rounded = probability.astype(jnp.bfloat16)
    attended = jnp.einsum(
        "hts,sd->thd", prob_rounded, value_rows, preferred_element_type=jnp.float32
    )
    row_delta = jnp.sum(grad_block.astype(jnp.float32) * attended, axis=-1)
    prob_grad = jnp.einsum(
        "thd,sd->hts", grad_block, value_rows, preferred_element_type=jnp.float32
    )
    score_rounded = (probability * (prob_grad - row_delta.T[:, :, None])).astype(jnp.bfloat16)
    key_term = (
        jnp.einsum("hts,thd->sd", score_rounded, query_block, preferred_element_type=jnp.float32)
        * score_scale
    )
    value_term = jnp.einsum(
        "hts,thd->sd", prob_rounded, grad_block, preferred_element_type=jnp.float32
    )
    return (score_rounded, key_term, value_term)


def shards(layer_input, queries, key_value, out_grad, segment_ids):
    tok_rows = queries.shape[0]
    head_width = key_value.shape[1]
    group_count = queries.shape[1] // head_width // 2
    score_scale = head_width ** (-0.5)
    partner = partner_2(key_value, "tensor", 0)
    is_even = lax.axis_index("tensor") % 2 == 0
    key_rows = jnp.where(is_even, key_value, partner)
    value_rows = jnp.where(is_even, partner, key_value)
    position = jnp.arange(tok_rows)
    segment_row = segment_ids[0]
    allowed = (position[None, :] <= position[:, None]) & (
        segment_row[:, None] == segment_row[None, :]
    )
    query_blocks = queries.reshape(tok_rows, group_count, 2, head_width)
    grad_blocks = out_grad.reshape(tok_rows, group_count, 2, head_width)
    zero_grad = jnp.zeros((tok_rows, head_width), jnp.float32)

    def block_terms(block_index):
        query_block = lax.dynamic_index_in_dim(query_blocks, block_index, 1, keepdims=False)
        grad_block = lax.dynamic_index_in_dim(grad_blocks, block_index, 1, keepdims=False)
        return score_block(query_block, grad_block, key_rows, value_rows, allowed, score_scale)

    def stored_step(block_index, state_carry):
        score_buffer, key_grad, value_grad = state_carry
        score_rounded, key_term, value_term = block_terms(block_index)
        score_buffer = lax.dynamic_update_index_in_dim(score_buffer, score_rounded, block_index, 0)
        return (score_buffer, key_grad + key_term, value_grad + value_term)

    score_buffer, key_grad, value_grad = lax.fori_loop(
        0,
        group_count,
        stored_step,
        (jnp.zeros((group_count, 2, tok_rows, tok_rows), jnp.bfloat16), zero_grad, zero_grad),
    )
    tensor_count = lax.axis_size("tensor")
    stacked = jnp.concatenate([key_grad, value_grad], axis=1)
    every_part = lax.all_gather(stacked.astype(jnp.bfloat16), "tensor", axis=1, tiled=True).astype(
        stacked.dtype
    )
    summed_pairs = every_part.reshape(tok_rows, tensor_count // 2, 2, 2, head_width).sum(axis=2)
    all_grads = summed_pairs.astype(jnp.bfloat16).reshape(tok_rows, tensor_count * head_width)
    grad_pair = lax.dynamic_slice_in_dim(
        all_grads, lax.axis_index("tensor") * head_width, head_width, 1
    )
    query_full = (
        jnp.einsum("ghts,sd->tghd", score_buffer, key_rows, preferred_element_type=jnp.float32)
        * score_scale
    )
    grad_query = query_full.astype(jnp.bfloat16).reshape(tok_rows, queries.shape[1])
    sequences = lax.axis_size("dp")
    product = lax.dot_general(
        layer_input, all_grads, (((0,), (0,)), ((), ())), preferred_element_type=jnp.float32
    )
    weight_grad = lax.psum_scatter(
        (product / sequences).astype(jnp.bfloat16), "dp", scatter_dimension=0, tiled=True
    )
    return (grad_query, grad_pair, weight_grad)


def solution(mesh):
    nd, nt_dev = mesh.shape["dp"], mesh.shape["tensor"]

    def body(layer_input, queries, key_value, out_grad, segment_ids):
        feat = layer_input.shape[1] // nd
        if feat % 128 or nd % 4 or nt_dev % 2:
            return shards(layer_input, queries, key_value, out_grad, segment_ids)
        return fused(nd, nt_dev, layer_input, queries, key_value, out_grad, segment_ids)

    return jax.shard_map(
        body,
        mesh=mesh,
        in_specs=(
            P("dp", "tensor"),
            P("dp", "tensor"),
            P("dp", "tensor"),
            P("dp", "tensor"),
            P("dp", None),
        ),
        out_specs=(P("dp", "tensor"), P("dp", "tensor"), P(("tensor", "dp"), None)),
        check_vma=False,
    )
```

```python
import functools
import math
import jax
import jax.numpy as jnp
from jax import lax
from jax.experimental import pallas as pl
from jax.experimental.pallas import tpu as pltpu
from jax.sharding import PartitionSpec as P

F32 = jnp.float32
BF16 = jnp.bfloat16


def nt(a, b):
    return lax.dot_general(a, b, (((1,), (1,)), ((), ())), preferred_element_type=F32)


def nn(a, b):
    return lax.dot_general(a, b, (((1,), (0,)), ((), ())), preferred_element_type=F32)


def tn(a, b):
    return lax.dot_general(a, b, (((0,), (0,)), ((), ())), preferred_element_type=F32)


def kernel(
    nd,
    nt_dev,
    feat,
    li_hbm,
    q_ref,
    kv_ref,
    og_ref,
    seg_ref,
    dq_ref,
    gkv_ref,
    gw_ref,
    kv_in,
    bias,
    kt,
    acc_k,
    acc_v,
    part_out,
    part_in,
    gbuf,
    li,
    pacc,
    sbuf,
    rbuf,
    kv_sem,
    lo_sem,
    ls_sem,
    lr_sem,
    px_sem,
    y_sem,
    fwd_sem,
    loc_sem,
    xs_sem,
    xr_sem,
    cs_sem,
    cr_sem,
):
    tok, hd = kv_ref.shape
    heads = q_ref.shape[1] // hd
    n = nd // 2
    groups = nt_dev // 2
    dp = lax.axis_index("dp")
    te = lax.axis_index("tensor")
    z = dp // 2
    y = dp % 2
    c = te % 2
    grp = te // 2
    other_y = z * 2 + 1 - y
    mate = grp * 2 + 1 - c

    def remote(src, dst, ssem, rsem, d, t):
        return pltpu.make_async_remote_copy(
            src_ref=src,
            dst_ref=dst,
            send_sem=ssem,
            recv_sem=rsem,
            device_id={"dp": d, "tensor": t},
            device_id_type=pl.DeviceIdType.MESH,
        )

    barrier = pltpu.get_barrier_semaphore()
    pl.semaphore_signal(
        barrier, inc=1, device_id={"dp": other_y, "tensor": te}, device_id_type=pl.DeviceIdType.MESH
    )
    for step in (1, n - 1):
        pl.semaphore_signal(
            barrier,
            inc=1,
            device_id={"dp": ((z + step) % n) * 2 + y, "tensor": te},
            device_id_type=pl.DeviceIdType.MESH,
        )
    for step in range(1, nt_dev):
        pl.semaphore_signal(
            barrier,
            inc=1,
            device_id={"dp": dp, "tensor": (te + step) % nt_dev},
            device_id_type=pl.DeviceIdType.MESH,
        )
    pl.semaphore_wait(barrier, 3 + nt_dev - 1)

    kv_copy = remote(kv_ref, kv_in, kv_sem.at[0], kv_sem.at[1], dp, mate)
    kv_copy.start()

    def feat_at(zz, yy):
        return li_hbm.at[:, pl.ds(pl.multiple_of((zz * 2 + yy) * feat, feat), feat)]

    def li_remote(zz):
        return remote(
            feat_at(zz, 1 - y),
            li.at[zz, pl.ds(tok, tok), :],
            ls_sem.at[zz],
            lr_sem.at[zz],
            other_y,
            te,
        )

    def li_local(zz):
        return pltpu.make_async_copy(feat_at(zz, y), li.at[zz, pl.ds(0, tok), :], lo_sem.at[zz])

    def li_order(k):
        low = n - 1 - k
        low = jnp.where(low <= z, low - 1, low)
        high = jnp.where(k >= z, k + 1, k)
        v = jnp.where(z < n // 2, low, high)
        return jnp.where(k == n - 1, z, v)

    li_remote(li_order(0)).start()
    for k in range(n):
        li_local(k).start()

    seg_b = jnp.broadcast_to(seg_ref[...].astype(F32), (tok, tok))
    key_pos = lax.broadcasted_iota(jnp.int32, (tok, tok), 0)
    qry_pos = lax.broadcasted_iota(jnp.int32, (tok, tok), 1)
    allowed = (key_pos <= qry_pos) & (seg_b.T == seg_b)
    bias[...] = jnp.where(allowed, 0.0, -1e30).astype(F32)
    acc_k[...] = jnp.zeros_like(acc_k)
    acc_v[...] = jnp.zeros_like(acc_v)
    kv_copy.wait()
    even = c == 0
    keys = jnp.where(even, kv_ref[...], kv_in[...])
    values = jnp.where(even, kv_in[...], kv_ref[...])
    scale = hd**-0.5
    coef = scale * math.log2(math.e)
    kt[0] = keys
    kt[1] = values
    keys_t = keys.astype(F32).T.astype(BF16)
    blk = tok // 2

    def head(h, carry):
        cols = pl.ds(pl.multiple_of(h * hd, hd), hd)
        for b in range(2):
            rows = pl.ds(b * blk, blk)
            kc = (b + 1) * blk
            q = q_ref[rows, cols]
            o = og_ref[rows, cols]
            s = nt(kt[0, 0:kc, :], q) * coef + bias[0:kc, rows]
            m = jnp.max(s, axis=0, keepdims=True)
            w = jnp.exp2(s - m)
            inv = 1.0 / jnp.sum(w, axis=0, keepdims=True)
            prob = w * inv
            pb = prob.astype(BF16)
            dpr = nt(kt[1, 0:kc, :], o)
            delta = jnp.sum(pb.astype(F32) * dpr, axis=0, keepdims=True)
            ds = (prob * (dpr - delta)).astype(BF16)
            acc_v[0:kc, :] += nn(pb, o)
            acc_k[0:kc, :] += nn(ds, q)
            dqt = nn(keys_t[:, 0:kc], ds) * scale
            dq_ref[rows, cols] = dqt.T.astype(BF16)
        return carry

    lax.fori_loop(0, heads, head, 0)

    def li_next(k):
        li_remote(li_order(k - 1)).wait_send()
        li_remote(li_order(k)).start()

    li_next(1)
    dk = acc_k[...] * scale
    dv = acc_v[...]
    part_out[...] = jnp.where(even, dv, dk).astype(BF16)
    px = remote(part_out, part_in, px_sem.at[0], px_sem.at[1], dp, mate)
    px.start()
    mine = jnp.where(even, dk, dv)
    px.wait()
    gkv_ref[...] = (mine + part_in[...].astype(F32)).astype(BF16)

    def cell(r, half, core):
        lanes = pl.ds(pl.multiple_of(core * hd, hd), hd)
        return gbuf.at[r, pl.ds(half * tok, tok), lanes]

    own = pltpu.make_async_copy(gkv_ref, cell(0, 0, c), loc_sem)
    own.start()
    y_copy = remote(gkv_ref, cell(0, 1, c), y_sem.at[0], y_sem.at[1], other_y, te)
    y_copy.start()
    fwd0 = remote(gkv_ref, cell(0, 0, c), fwd_sem.at[0, 0], fwd_sem.at[1, 0], dp, mate)
    fwd0.start()

    def x_copy(r, core, half, src):
        back = groups - r
        return remote(
            src,
            cell(back, half, c),
            xs_sem.at[r, core, half],
            xr_sem.at[back, c, half],
            dp,
            ((grp + r) % groups) * 2 + core,
        )

    for r in range(1, groups):
        for core in range(2):
            x_copy(r, core, 0, gkv_ref).start()
    y_copy.wait_recv()
    fwd1 = remote(cell(0, 1, c), cell(0, 1, c), fwd_sem.at[0, 1], fwd_sem.at[1, 1], dp, mate)
    fwd1.start()
    for r in range(1, groups):
        for core in range(2):
            x_copy(r, core, 1, cell(0, 1, c)).start()
    own.wait()
    y_copy.wait_send()
    for half, copy in ((0, fwd0), (1, fwd1)):
        copy.wait_send()
        land = cell(0, half, 1 - c)
        remote(land, land, fwd_sem.at[0, half], fwd_sem.at[1, half], dp, mate).wait_recv()

    inv_seq = 1.0 / nd

    def product(r, zz):
        pacc[...] = tn(li[zz], gbuf[r]) * inv_seq

    def chain(side, r, zz):
        step = 1 if side == 0 else -1
        return remote(
            sbuf.at[side, r, zz],
            rbuf.at[side, r, zz],
            cs_sem.at[side, r, zz],
            cr_sem.at[side, r, zz],
            (z + step) * 2 + y,
            te,
        )

    def li_wait(zz):
        li_local(zz).wait()
        li_remote(zz).wait_recv()

    def arrived(side, r, zz):
        return remote(
            sbuf.at[side, r, zz],
            rbuf.at[side, r, zz],
            cs_sem.at[side, r, zz],
            cr_sem.at[side, r, zz],
            ((z + 1) % n) * 2 + y,
            te,
        )

    def hop(side, r, zz):
        product(r, zz)
        inner = (z > 0) if side == 0 else (z < n - 1)

        @pl.when(inner)
        def _():
            arrived(side, r, zz).wait_recv()
            pacc[...] += rbuf[side, r, zz].astype(F32)

        sbuf[side, r, zz] = pacc[...].astype(BF16)
        chain(side, r, zz).start()

    def dist_step(k, carry):
        zz = li_order(k)
        li_wait(zz)

        @pl.when(k < n - 2)
        def _():
            li_next(k + 2)

        def group_step(r, carry):
            @pl.when((k == 0) & (r > 0))
            def _():
                for core in range(2):
                    for half in range(2):
                        land = cell(r, half, core)
                        remote(
                            land, land, xs_sem.at[r, core, half], xr_sem.at[r, core, half], dp, mate
                        ).wait_recv()

            @pl.when(zz > z)
            def _():
                hop(0, r, zz)

            @pl.when(zz < z)
            def _():
                hop(1, r, zz)

            return carry

        return lax.fori_loop(0, groups, group_step, carry)

    lax.fori_loop(0, n - 1, dist_step, 0)

    li_wait(z)

    def finish(r, carry):
        product(r, z)

        @pl.when(z > 0)
        def _():
            arrived(0, r, z).wait_recv()
            pacc[...] += rbuf[0, r, z].astype(F32)

        @pl.when(z < n - 1)
        def _():
            arrived(1, r, z).wait_recv()
            pacc[...] += rbuf[1, r, z].astype(F32)

        width = 2 * hd
        at = pl.multiple_of(((grp + r) % groups) * width, width)
        gw_ref[:, pl.ds(at, width)] = pacc[...].astype(BF16)
        return carry

    lax.fori_loop(0, groups, finish, 0)

    li_remote(z).wait_send()
    for r in range(1, groups):
        for core in range(2):
            for half in range(2):
                x_copy(r, core, half, cell(0, half, c)).wait_send()

    def drain(r, carry):
        def drain_step(k, carry):
            right = n - 1 - k

            @pl.when(right > z)
            def _():
                arrived(0, r, right).wait_send()

            @pl.when(k < z)
            def _():
                arrived(1, r, k).wait_send()

            return carry

        return lax.fori_loop(0, n - 1, drain_step, carry)

    lax.fori_loop(0, groups, drain, 0)


def fused(nd, nt_dev, layer_input, queries, key_value, out_grad, segment_ids):
    tok, hd = key_value.shape
    feat = layer_input.shape[1] // nd
    n, groups = nd // 2, nt_dev // 2
    width = 2 * hd
    vmem = pl.BlockSpec(memory_space=pltpu.VMEM)
    dma = pltpu.SemaphoreType.DMA
    return pl.pallas_call(
        functools.partial(kernel, nd, nt_dev, feat),
        out_shape=(
            jax.ShapeDtypeStruct(queries.shape, BF16),
            jax.ShapeDtypeStruct(key_value.shape, BF16),
            jax.ShapeDtypeStruct((feat, width * groups), BF16),
        ),
        in_specs=[pl.BlockSpec(memory_space=pl.ANY), vmem, vmem, vmem, vmem],
        out_specs=(vmem, vmem, vmem),
        scratch_shapes=[
            pltpu.VMEM((tok, hd), BF16),
            pltpu.VMEM((tok, tok), F32),
            pltpu.VMEM((2, tok, hd), BF16),
            pltpu.VMEM((tok, hd), F32),
            pltpu.VMEM((tok, hd), F32),
            pltpu.VMEM((tok, hd), BF16),
            pltpu.VMEM((tok, hd), BF16),
            pltpu.VMEM((groups, 2 * tok, width), BF16),
            pltpu.VMEM((n, 2 * tok, feat), BF16),
            pltpu.VMEM((feat, width), F32),
            pltpu.VMEM((2, groups, n, feat, width), BF16),
            pltpu.VMEM((2, groups, n, feat, width), BF16),
            dma((2,)),
            dma((n,)),
            dma((n,)),
            dma((n,)),
            dma((2,)),
            dma((2,)),
            dma((2, 2)),
            dma,
            dma((groups, 2, 2)),
            dma((groups, 2, 2)),
            dma((2, groups, n)),
            dma((2, groups, n)),
        ],
        compiler_params=pltpu.CompilerParams(
            collective_id=0, has_side_effects=True, vmem_limit_bytes=56 * 2**20
        ),
    )(layer_input, queries, key_value, out_grad, segment_ids)


def partner_2(value, axis, stride):
    mask = 2**stride
    pairs = [(source, source ^ mask) for source in range(lax.axis_size(axis))]
    return lax.ppermute(value, axis, pairs)


def score_block(query_block, grad_block, key_rows, value_rows, allowed, score_scale):
    scores = (
        jnp.einsum("thd,sd->hts", query_block, key_rows, preferred_element_type=jnp.float32)
        * score_scale
    )
    scores = jnp.where(allowed[None], scores, -1e30)
    row_max = jnp.max(scores, axis=-1, keepdims=True)
    weights = jnp.exp(scores - row_max)
    probability = weights / jnp.sum(weights, axis=-1, keepdims=True)
    prob_rounded = probability.astype(jnp.bfloat16)
    attended = jnp.einsum(
        "hts,sd->thd", prob_rounded, value_rows, preferred_element_type=jnp.float32
    )
    row_delta = jnp.sum(grad_block.astype(jnp.float32) * attended, axis=-1)
    prob_grad = jnp.einsum(
        "thd,sd->hts", grad_block, value_rows, preferred_element_type=jnp.float32
    )
    score_rounded = (probability * (prob_grad - row_delta.T[:, :, None])).astype(jnp.bfloat16)
    key_term = (
        jnp.einsum("hts,thd->sd", score_rounded, query_block, preferred_element_type=jnp.float32)
        * score_scale
    )
    value_term = jnp.einsum(
        "hts,thd->sd", prob_rounded, grad_block, preferred_element_type=jnp.float32
    )
    return (score_rounded, key_term, value_term)


def shards(layer_input, queries, key_value, out_grad, segment_ids):
    tok_rows = queries.shape[0]
    head_width = key_value.shape[1]
    group_count = queries.shape[1] // head_width // 2
    score_scale = head_width ** (-0.5)
    partner = partner_2(key_value, "tensor", 0)
    is_even = lax.axis_index("tensor") % 2 == 0
    key_rows = jnp.where(is_even, key_value, partner)
    value_rows = jnp.where(is_even, partner, key_value)
    position = jnp.arange(tok_rows)
    segment_row = segment_ids[0]
    allowed = (position[None, :] <= position[:, None]) & (
        segment_row[:, None] == segment_row[None, :]
    )
    query_blocks = queries.reshape(tok_rows, group_count, 2, head_width)
    grad_blocks = out_grad.reshape(tok_rows, group_count, 2, head_width)
    zero_grad = jnp.zeros((tok_rows, head_width), jnp.float32)

    def block_terms(block_index):
        query_block = lax.dynamic_index_in_dim(query_blocks, block_index, 1, keepdims=False)
        grad_block = lax.dynamic_index_in_dim(grad_blocks, block_index, 1, keepdims=False)
        return score_block(query_block, grad_block, key_rows, value_rows, allowed, score_scale)

    def stored_step(block_index, state_carry):
        score_buffer, key_grad, value_grad = state_carry
        score_rounded, key_term, value_term = block_terms(block_index)
        score_buffer = lax.dynamic_update_index_in_dim(score_buffer, score_rounded, block_index, 0)
        return (score_buffer, key_grad + key_term, value_grad + value_term)

    score_buffer, key_grad, value_grad = lax.fori_loop(
        0,
        group_count,
        stored_step,
        (jnp.zeros((group_count, 2, tok_rows, tok_rows), jnp.bfloat16), zero_grad, zero_grad),
    )
    tensor_count = lax.axis_size("tensor")
    stacked = jnp.concatenate([key_grad, value_grad], axis=1)
    every_part = lax.all_gather(stacked.astype(jnp.bfloat16), "tensor", axis=1, tiled=True).astype(
        stacked.dtype
    )
    summed_pairs = every_part.reshape(tok_rows, tensor_count // 2, 2, 2, head_width).sum(axis=2)
    all_grads = summed_pairs.astype(jnp.bfloat16).reshape(tok_rows, tensor_count * head_width)
    grad_pair = lax.dynamic_slice_in_dim(
        all_grads, lax.axis_index("tensor") * head_width, head_width, 1
    )
    query_full = (
        jnp.einsum("ghts,sd->tghd", score_buffer, key_rows, preferred_element_type=jnp.float32)
        * score_scale
    )
    grad_query = query_full.astype(jnp.bfloat16).reshape(tok_rows, queries.shape[1])
    sequences = lax.axis_size("dp")
    product = lax.dot_general(
        layer_input, all_grads, (((0,), (0,)), ((), ())), preferred_element_type=jnp.float32
    )
    weight_grad = lax.psum_scatter(
        (product / sequences).astype(jnp.bfloat16), "dp", scatter_dimension=0, tiled=True
    )
    return (grad_query, grad_pair, weight_grad)


def solution(mesh):
    nd, nt_dev = mesh.shape["dp"], mesh.shape["tensor"]

    def body(layer_input, queries, key_value, out_grad, segment_ids):
        feat = layer_input.shape[1] // nd
        if feat % 128 or nd % 4 or nt_dev % 2:
            return shards(layer_input, queries, key_value, out_grad, segment_ids)
        return fused(nd, nt_dev, layer_input, queries, key_value, out_grad, segment_ids)

    return jax.shard_map(
        body,
        mesh=mesh,
        in_specs=(
            P("dp", "tensor"),
            P("dp", "tensor"),
            P("dp", "tensor"),
            P("dp", "tensor"),
            P("dp", None),
        ),
        out_specs=(P("dp", "tensor"), P("dp", "tensor"), P(("tensor", "dp"), None)),
        check_vma=False,
    )
```

```python
import functools
import math
import jax
import jax.numpy as jnp
from jax import lax
from jax.experimental import pallas as pl
from jax.experimental.pallas import tpu as pltpu
from jax.sharding import PartitionSpec as P

F32 = jnp.float32
BF16 = jnp.bfloat16


def nt(a, b):
    return lax.dot_general(a, b, (((1,), (1,)), ((), ())), preferred_element_type=F32)


def nn(a, b):
    return lax.dot_general(a, b, (((1,), (0,)), ((), ())), preferred_element_type=F32)


def tn(a, b):
    return lax.dot_general(a, b, (((0,), (0,)), ((), ())), preferred_element_type=F32)


def kernel(
    nd,
    nt_dev,
    feat,
    li_hbm,
    q_ref,
    kv_ref,
    og_ref,
    seg_ref,
    dq_ref,
    gkv_ref,
    gw_ref,
    kv_in,
    bias,
    kt,
    acc_k,
    acc_v,
    part_out,
    part_in,
    gbuf,
    li,
    pacc,
    sbuf,
    rbuf,
    kv_sem,
    lo_sem,
    ls_sem,
    lr_sem,
    px_sem,
    y_sem,
    fwd_sem,
    loc_sem,
    xs_sem,
    xr_sem,
    cs_sem,
    cr_sem,
):
    tok, hd = kv_ref.shape
    heads = q_ref.shape[1] // hd
    n = nd // 2
    groups = nt_dev // 2
    dp = lax.axis_index("dp")
    te = lax.axis_index("tensor")
    z = dp // 2
    y = dp % 2
    c = te % 2
    grp = te // 2
    other_y = z * 2 + 1 - y
    mate = grp * 2 + 1 - c

    def remote(src, dst, ssem, rsem, d, t):
        return pltpu.make_async_remote_copy(
            src_ref=src,
            dst_ref=dst,
            send_sem=ssem,
            recv_sem=rsem,
            device_id={"dp": d, "tensor": t},
            device_id_type=pl.DeviceIdType.MESH,
        )

    barrier = pltpu.get_barrier_semaphore()
    pl.semaphore_signal(
        barrier, inc=1, device_id={"dp": other_y, "tensor": te}, device_id_type=pl.DeviceIdType.MESH
    )
    for step in (1, n - 1):
        pl.semaphore_signal(
            barrier,
            inc=1,
            device_id={"dp": ((z + step) % n) * 2 + y, "tensor": te},
            device_id_type=pl.DeviceIdType.MESH,
        )
    for step in range(1, nt_dev):
        pl.semaphore_signal(
            barrier,
            inc=1,
            device_id={"dp": dp, "tensor": (te + step) % nt_dev},
            device_id_type=pl.DeviceIdType.MESH,
        )
    pl.semaphore_wait(barrier, 3 + nt_dev - 1)

    kv_copy = remote(kv_ref, kv_in, kv_sem.at[0], kv_sem.at[1], dp, mate)
    kv_copy.start()

    def feat_at(zz, yy):
        return li_hbm.at[:, pl.ds(pl.multiple_of((zz * 2 + yy) * feat, feat), feat)]

    def li_remote(zz):
        return remote(
            feat_at(zz, 1 - y),
            li.at[zz, pl.ds(tok, tok), :],
            ls_sem.at[zz],
            lr_sem.at[zz],
            other_y,
            te,
        )

    def li_local(zz):
        return pltpu.make_async_copy(feat_at(zz, y), li.at[zz, pl.ds(0, tok), :], lo_sem.at[zz])

    def li_order(k):
        low = n - 1 - k
        low = jnp.where(low <= z, low - 1, low)
        high = jnp.where(k >= z, k + 1, k)
        v = jnp.where(z < n // 2, low, high)
        return jnp.where(k == n - 1, z, v)

    li_remote(li_order(0)).start()
    for k in range(n):
        li_local(k).start()

    seg_b = jnp.broadcast_to(seg_ref[...].astype(F32), (tok, tok))
    key_pos = lax.broadcasted_iota(jnp.int32, (tok, tok), 0)
    qry_pos = lax.broadcasted_iota(jnp.int32, (tok, tok), 1)
    allowed = (key_pos <= qry_pos) & (seg_b.T == seg_b)
    bias[...] = jnp.where(allowed, 0.0, -1e30).astype(F32)
    acc_k[...] = jnp.zeros_like(acc_k)
    acc_v[...] = jnp.zeros_like(acc_v)
    kv_copy.wait()
    even = c == 0
    keys = jnp.where(even, kv_ref[...], kv_in[...])
    values = jnp.where(even, kv_in[...], kv_ref[...])
    scale = hd**-0.5
    coef = scale * math.log2(math.e)
    kt[0] = keys
    kt[1] = values
    keys_t = keys.astype(F32).T.astype(BF16)
    blk = tok // 2

    def head(h, carry):
        cols = pl.ds(pl.multiple_of(h * hd, hd), hd)
        for b in range(2):
            rows = pl.ds(b * blk, blk)
            kc = (b + 1) * blk
            q = q_ref[rows, cols]
            o = og_ref[rows, cols]
            s = nt(kt[0, 0:kc, :], q) * coef + bias[0:kc, rows]
            m = jnp.max(s, axis=0, keepdims=True)
            w = jnp.exp2(s - m)
            inv = 1.0 / jnp.sum(w, axis=0, keepdims=True)
            prob = w * inv
            pb = prob.astype(BF16)
            dpr = nt(kt[1, 0:kc, :], o)
            delta = jnp.sum(pb.astype(F32) * dpr, axis=0, keepdims=True)
            ds = (prob * (dpr - delta)).astype(BF16)
            acc_v[0:kc, :] += nn(pb, o)
            acc_k[0:kc, :] += nn(ds, q)
            dqt = nn(keys_t[:, 0:kc], ds) * scale
            dq_ref[rows, cols] = dqt.T.astype(BF16)
        return carry

    lax.fori_loop(0, heads, head, 0)

    def li_next(k):
        li_remote(li_order(k - 1)).wait_send()
        li_remote(li_order(k)).start()

    li_next(1)
    dk = acc_k[...] * scale
    dv = acc_v[...]
    part_out[...] = jnp.where(even, dv, dk).astype(BF16)
    px = remote(part_out, part_in, px_sem.at[0], px_sem.at[1], dp, mate)
    px.start()
    mine = jnp.where(even, dk, dv)
    px.wait()
    gkv_ref[...] = (mine + part_in[...].astype(F32)).astype(BF16)

    def cell(r, half, core):
        lanes = pl.ds(pl.multiple_of(core * hd, hd), hd)
        return gbuf.at[r, pl.ds(half * tok, tok), lanes]

    own = pltpu.make_async_copy(gkv_ref, cell(0, 0, c), loc_sem)
    own.start()
    y_copy = remote(gkv_ref, cell(0, 1, c), y_sem.at[0], y_sem.at[1], other_y, te)
    y_copy.start()
    fwd0 = remote(gkv_ref, cell(0, 0, c), fwd_sem.at[0, 0], fwd_sem.at[1, 0], dp, mate)
    fwd0.start()

    def x_copy(r, core, half, src):
        back = groups - r
        return remote(
            src,
            cell(back, half, c),
            xs_sem.at[r, core, half],
            xr_sem.at[back, c, half],
            dp,
            ((grp + r) % groups) * 2 + core,
        )

    for r in range(1, groups):
        for core in range(2):
            x_copy(r, core, 0, gkv_ref).start()
    y_copy.wait_recv()
    fwd1 = remote(cell(0, 1, c), cell(0, 1, c), fwd_sem.at[0, 1], fwd_sem.at[1, 1], dp, mate)
    fwd1.start()
    for r in range(1, groups):
        for core in range(2):
            x_copy(r, core, 1, cell(0, 1, c)).start()
    own.wait()
    y_copy.wait_send()
    for half, copy in ((0, fwd0), (1, fwd1)):
        copy.wait_send()
        land = cell(0, half, 1 - c)
        remote(land, land, fwd_sem.at[0, half], fwd_sem.at[1, half], dp, mate).wait_recv()

    inv_seq = 1.0 / nd

    def product(r, zz):
        pacc[...] = tn(li[zz], gbuf[r]) * inv_seq

    def chain(side, r, zz):
        step = 1 if side == 0 else -1
        return remote(
            sbuf.at[side, r, zz],
            rbuf.at[side, r, zz],
            cs_sem.at[side, r, zz],
            cr_sem.at[side, r, zz],
            (z + step) * 2 + y,
            te,
        )

    def li_wait(zz):
        li_local(zz).wait()
        li_remote(zz).wait_recv()

    def arrived(side, r, zz):
        return remote(
            sbuf.at[side, r, zz],
            rbuf.at[side, r, zz],
            cs_sem.at[side, r, zz],
            cr_sem.at[side, r, zz],
            ((z + 1) % n) * 2 + y,
            te,
        )

    def hop(side, r, zz):
        product(r, zz)
        inner = (z > 0) if side == 0 else (z < n - 1)

        @pl.when(inner)
        def _():
            arrived(side, r, zz).wait_recv()
            pacc[...] += rbuf[side, r, zz].astype(F32)

        sbuf[side, r, zz] = pacc[...].astype(BF16)
        chain(side, r, zz).start()

    def dist_step(k, carry):
        zz = li_order(k)
        li_wait(zz)

        @pl.when(k < n - 2)
        def _():
            li_next(k + 2)

        def group_step(r, carry):
            @pl.when((k == 0) & (r > 0))
            def _():
                for core in range(2):
                    for half in range(2):
                        land = cell(r, half, core)
                        remote(
                            land, land, xs_sem.at[r, core, half], xr_sem.at[r, core, half], dp, mate
                        ).wait_recv()

            @pl.when(zz > z)
            def _():
                hop(0, r, zz)

            @pl.when(zz < z)
            def _():
                hop(1, r, zz)

            return carry

        return lax.fori_loop(0, groups, group_step, carry)

    lax.fori_loop(0, n - 1, dist_step, 0)

    li_wait(z)

    def finish(r, carry):
        product(r, z)

        @pl.when(z > 0)
        def _():
            arrived(0, r, z).wait_recv()
            pacc[...] += rbuf[0, r, z].astype(F32)

        @pl.when(z < n - 1)
        def _():
            arrived(1, r, z).wait_recv()
            pacc[...] += rbuf[1, r, z].astype(F32)

        width = 2 * hd
        at = pl.multiple_of(((grp + r) % groups) * width, width)
        gw_ref[:, pl.ds(at, width)] = pacc[...].astype(BF16)
        return carry

    lax.fori_loop(0, groups, finish, 0)

    li_remote(z).wait_send()
    for r in range(1, groups):
        for core in range(2):
            for half in range(2):
                x_copy(r, core, half, cell(0, half, c)).wait_send()

    def drain(r, carry):
        def drain_step(k, carry):
            right = n - 1 - k

            @pl.when(right > z)
            def _():
                arrived(0, r, right).wait_send()

            @pl.when(k < z)
            def _():
                arrived(1, r, k).wait_send()

            return carry

        return lax.fori_loop(0, n - 1, drain_step, carry)

    lax.fori_loop(0, groups, drain, 0)


def fused(nd, nt_dev, layer_input, queries, key_value, out_grad, segment_ids):
    tok, hd = key_value.shape
    feat = layer_input.shape[1] // nd
    n, groups = nd // 2, nt_dev // 2
    width = 2 * hd
    vmem = pl.BlockSpec(memory_space=pltpu.VMEM)
    dma = pltpu.SemaphoreType.DMA
    return pl.pallas_call(
        functools.partial(kernel, nd, nt_dev, feat),
        out_shape=(
            jax.ShapeDtypeStruct(queries.shape, BF16),
            jax.ShapeDtypeStruct(key_value.shape, BF16),
            jax.ShapeDtypeStruct((feat, width * groups), BF16),
        ),
        in_specs=[pl.BlockSpec(memory_space=pl.ANY), vmem, vmem, vmem, vmem],
        out_specs=(vmem, vmem, vmem),
        scratch_shapes=[
            pltpu.VMEM((tok, hd), BF16),
            pltpu.VMEM((tok, tok), F32),
            pltpu.VMEM((2, tok, hd), BF16),
            pltpu.VMEM((tok, hd), F32),
            pltpu.VMEM((tok, hd), F32),
            pltpu.VMEM((tok, hd), BF16),
            pltpu.VMEM((tok, hd), BF16),
            pltpu.VMEM((groups, 2 * tok, width), BF16),
            pltpu.VMEM((n, 2 * tok, feat), BF16),
            pltpu.VMEM((feat, width), F32),
            pltpu.VMEM((2, groups, n, feat, width), BF16),
            pltpu.VMEM((2, groups, n, feat, width), BF16),
            dma((2,)),
            dma((n,)),
            dma((n,)),
            dma((n,)),
            dma((2,)),
            dma((2,)),
            dma((2, 2)),
            dma,
            dma((groups, 2, 2)),
            dma((groups, 2, 2)),
            dma((2, groups, n)),
            dma((2, groups, n)),
        ],
        compiler_params=pltpu.CompilerParams(
            collective_id=0, has_side_effects=True, vmem_limit_bytes=56 * 2**20
        ),
    )(layer_input, queries, key_value, out_grad, segment_ids)


def partner_2(value, axis, stride):
    mask = 2**stride
    pairs = [(source, source ^ mask) for source in range(lax.axis_size(axis))]
    return lax.ppermute(value, axis, pairs)


def score_block(query_block, grad_block, key_rows, value_rows, allowed, score_scale):
    scores = (
        jnp.einsum("thd,sd->hts", query_block, key_rows, preferred_element_type=jnp.float32)
        * score_scale
    )
    scores = jnp.where(allowed[None], scores, -1e30)
    row_max = jnp.max(scores, axis=-1, keepdims=True)
    weights = jnp.exp(scores - row_max)
    probability = weights / jnp.sum(weights, axis=-1, keepdims=True)
    prob_rounded = probability.astype(jnp.bfloat16)
    attended = jnp.einsum(
        "hts,sd->thd", prob_rounded, value_rows, preferred_element_type=jnp.float32
    )
    row_delta = jnp.sum(grad_block.astype(jnp.float32) * attended, axis=-1)
    prob_grad = jnp.einsum(
        "thd,sd->hts", grad_block, value_rows, preferred_element_type=jnp.float32
    )
    score_rounded = (probability * (prob_grad - row_delta.T[:, :, None])).astype(jnp.bfloat16)
    key_term = (
        jnp.einsum("hts,thd->sd", score_rounded, query_block, preferred_element_type=jnp.float32)
        * score_scale
    )
    value_term = jnp.einsum(
        "hts,thd->sd", prob_rounded, grad_block, preferred_element_type=jnp.float32
    )
    return (score_rounded, key_term, value_term)


def shards(layer_input, queries, key_value, out_grad, segment_ids):
    tok_rows = queries.shape[0]
    head_width = key_value.shape[1]
    group_count = queries.shape[1] // head_width // 2
    score_scale = head_width ** (-0.5)
    partner = partner_2(key_value, "tensor", 0)
    is_even = lax.axis_index("tensor") % 2 == 0
    key_rows = jnp.where(is_even, key_value, partner)
    value_rows = jnp.where(is_even, partner, key_value)
    position = jnp.arange(tok_rows)
    segment_row = segment_ids[0]
    allowed = (position[None, :] <= position[:, None]) & (
        segment_row[:, None] == segment_row[None, :]
    )
    query_blocks = queries.reshape(tok_rows, group_count, 2, head_width)
    grad_blocks = out_grad.reshape(tok_rows, group_count, 2, head_width)
    zero_grad = jnp.zeros((tok_rows, head_width), jnp.float32)

    def block_terms(block_index):
        query_block = lax.dynamic_index_in_dim(query_blocks, block_index, 1, keepdims=False)
        grad_block = lax.dynamic_index_in_dim(grad_blocks, block_index, 1, keepdims=False)
        return score_block(query_block, grad_block, key_rows, value_rows, allowed, score_scale)

    def stored_step(block_index, state_carry):
        score_buffer, key_grad, value_grad = state_carry
        score_rounded, key_term, value_term = block_terms(block_index)
        score_buffer = lax.dynamic_update_index_in_dim(score_buffer, score_rounded, block_index, 0)
        return (score_buffer, key_grad + key_term, value_grad + value_term)

    score_buffer, key_grad, value_grad = lax.fori_loop(
        0,
        group_count,
        stored_step,
        (jnp.zeros((group_count, 2, tok_rows, tok_rows), jnp.bfloat16), zero_grad, zero_grad),
    )
    tensor_count = lax.axis_size("tensor")
    stacked = jnp.concatenate([key_grad, value_grad], axis=1)
    every_part = lax.all_gather(stacked.astype(jnp.bfloat16), "tensor", axis=1, tiled=True).astype(
        stacked.dtype
    )
    summed_pairs = every_part.reshape(tok_rows, tensor_count // 2, 2, 2, head_width).sum(axis=2)
    all_grads = summed_pairs.astype(jnp.bfloat16).reshape(tok_rows, tensor_count * head_width)
    grad_pair = lax.dynamic_slice_in_dim(
        all_grads, lax.axis_index("tensor") * head_width, head_width, 1
    )
    query_full = (
        jnp.einsum("ghts,sd->tghd", score_buffer, key_rows, preferred_element_type=jnp.float32)
        * score_scale
    )
    grad_query = query_full.astype(jnp.bfloat16).reshape(tok_rows, queries.shape[1])
    sequences = lax.axis_size("dp")
    product = lax.dot_general(
        layer_input, all_grads, (((0,), (0,)), ((), ())), preferred_element_type=jnp.float32
    )
    weight_grad = lax.psum_scatter(
        (product / sequences).astype(jnp.bfloat16), "dp", scatter_dimension=0, tiled=True
    )
    return (grad_query, grad_pair, weight_grad)


def move(*refs):
    count = (len(refs) - 1) // 2
    sem = refs[-1]
    copies = [
        pltpu.make_async_copy(refs[i], refs[count + i], sem.at[i]) for i in range(count)
    ]
    for copy in copies:
        copy.start()
    for copy in copies:
        copy.wait()


def settle(results):
    anywhere = pl.BlockSpec(memory_space=pl.ANY)
    return pl.pallas_call(
        move,
        out_shape=tuple(jax.ShapeDtypeStruct(v.shape, v.dtype) for v in results),
        in_specs=[pl.BlockSpec(memory_space=pltpu.VMEM)] * len(results),
        out_specs=(anywhere,) * len(results),
        scratch_shapes=[pltpu.SemaphoreType.DMA((len(results),))],
    )(*results)


def solution(mesh):
    nd, nt_dev = mesh.shape["dp"], mesh.shape["tensor"]

    def body(layer_input, queries, key_value, out_grad, segment_ids):
        feat = layer_input.shape[1] // nd
        if feat % 128 or nd % 4 or nt_dev % 2:
            return shards(layer_input, queries, key_value, out_grad, segment_ids)
        return settle(fused(nd, nt_dev, layer_input, queries, key_value, out_grad, segment_ids))

    return jax.shard_map(
        body,
        mesh=mesh,
        in_specs=(
            P("dp", "tensor"),
            P("dp", "tensor"),
            P("dp", "tensor"),
            P("dp", "tensor"),
            P("dp", None),
        ),
        out_specs=(P("dp", "tensor"), P("dp", "tensor"), P(("tensor", "dp"), None)),
        check_vma=False,
    )
```
